512 devices in a mesh: replica: 32 (over x, y), table: 16 (over z, core).
Axes of the slice: x: 4, y: 8, z: 8, core: 2. Of those that a mesh axis runs over, the one named last changes fastest.
Arguments:
- emb_table: float32 [16384, 128], P('table'), may hold values from -3 to 3
- row_accum: float32 [16384], P('table'), may hold values from 0.001 to 1
- look_rows: int32 [32, 16, 16, 4, 312], P('replica', 'table'), may hold values from 0 to 1023
- live_counts: int32 [32, 16, 16], P('replica'), may hold values from 1 to 312, 3328 in all within a row
- bag_order: int32 [32, 16, 3328], P('replica', 'table'), may hold values from 0 to 3327, each once within a row
- dense_emb: bfloat16 [65536, 128], P(('replica', 'table')), may hold values from -6 to 6
- labels: int32 [65536], P(('replica', 'table')), may hold values 0 or 1
- cross_in: bfloat16 [3456, 512], P('table'), may hold values from -0.109375 to 0.109375
- cross_out: bfloat16 [3456, 512], P('table'), may hold values from -0.25 to 0.25
- cross_bias: float32 [3456], replicated, may hold values from -3 to 3
- head_weight: float32 [3456], replicated, may hold values from -0.109375 to 0.109375
Outputs:
- logits: float32 [65536], P(('replica', 'table'))
- row_update: float32 [16384, 128], P('table')
- new_accum: float32 [16384], P('table')
The draws below stay inside these ranges and needn't reach their ends.
Inputs may be any that keep to these rules, and one draw needn't show every extreme that they name: `look_rows`: local row numbers within shard s; entries in unused slots are ignored. `live_counts`: for each replica and owner the counts over shards sum to 3328; for each of them some shard sends exactly 312. `bag_order`: each of an owner's 3328 bags appears once.
All inputs are finite; a program needn't handle non-finite values. No bound on the sum of `labels` on one device may be relied on, other than what follows from the above.
Results may differ from the reference program's by a relative error of at most 0.0045.
Values may be sent and summed in bfloat16 or wider, within the bound.
A program may use at most 64 MiB of HBM per device.

```python
import math
import jax
import jax.numpy as jnp
import numpy as np
from jax import lax

E = 128
RANK = 512
HOT = 4
ROWS_DEV = 1024
D = 3456
K = 3328
CAP = 312
SAMPLES = 65536
VOCAB = 16384
N_REPLICA = 32
N_TABLE = 16


def touch_ends(array, rng, smallest, largest):
    longest = array.shape.index(max(array.shape))
    spots = []
    for shift in (0, 1):
        where = [jax.random.randint(jax.random.fold_in(rng, axis), (), 0, length) for axis, length in enumerate(array.shape)]
        where[longest] = (where[longest] + shift) % array.shape[longest]
        spots.append(tuple(where))
    return array.at[spots[0]].set(smallest).at[spots[1]].set(largest)


def shard_levels(rng, extent, cuts, least, high):
    def one(dim, parts):
        draws = jax.random.uniform(jax.random.fold_in(jax.random.fold_in(rng, 6), dim), (parts,), jnp.float32, least / len(cuts), high / len(cuts))
        return jnp.repeat(jnp.exp(draws), extent[dim] // parts).reshape((-1,) + (1,) * (len(extent) - dim - 1))

    factor_of = one(*cuts[0])
    for cut in cuts[1:]:
        factor_of = factor_of * one(*cut)
    return factor_of


def rank_bounds(amount, lean):
    weights = [(1 << 20) // math.isqrt(standing ** lean) + 1 for standing in range(1, amount + 1)]
    width = 1 + sum(weights) // (1 << 30)
    return np.cumsum(np.array([max(1, weight // width) for weight in weights]))


def ranked(stream_key, extent, number_of, slope):
    grid = rank_bounds(number_of, slope)
    pick = jax.random.randint(jax.random.fold_in(stream_key, 1), extent, 0, int(grid[number_of - 1]))
    standing = jnp.searchsorted(jnp.asarray(grid, jnp.int32), pick, side="right")
    return jax.random.permutation(jax.random.fold_in(stream_key, 2), number_of)[standing].astype(jnp.int32)


def profile(number_of, total, limit, slope):
    weights = [(1 << 20) // math.isqrt(grade ** slope) + 1 for grade in range(2, number_of + 1)]
    surplus, counts = total - limit - (number_of - 1), [1] * (number_of - 1)
    while surplus > 0:
        candidates = [i for i in range(number_of - 1) if counts[i] < limit]
        pool, remaining = sum([weights[i] for i in candidates]), surplus
        for i in candidates:
            more = min(limit - counts[i], max(1, remaining * weights[i] // pool), surplus)
            counts[i] = counts[i] + more
            surplus = surplus - more
    return np.array([limit] + counts)


def ragged(own_key, number_of, total, reach, slope):
    if number_of == 2:
        one = jax.random.randint(own_key, (), max(1, total - reach), min(reach, total - 1) + 1)
        return jnp.stack([one, total - one])
    tallies = jnp.asarray(profile(number_of, total, reach, slope), jnp.int32)
    couples = (number_of - 1) // 2
    donor, sink = tallies[1:1 + 2 * couples:2], tallies[2:2 + 2 * couples:2]
    slack = jnp.minimum(donor - 1, reach - sink)
    moved = jax.random.randint(jax.random.fold_in(own_key, 1), (couples,), 0, 1 << 20) % (slack + 1)
    tallies = tallies.at[1:1 + 2 * couples:2].set(donor - moved).at[2:2 + 2 * couples:2].set(sink + moved)
    return tallies[jax.random.permutation(jax.random.fold_in(own_key, 2), number_of)]


def centred(own_key, dims, width, bound, cuts=(), held_as=jnp.bfloat16):
    values = jax.random.normal(own_key, dims, jnp.float32) * width
    if len(cuts) > 0:
        values = shard_levels(own_key, dims, cuts, -0.22, 0.18) * values
    return jnp.clip(values, min=-bound, max=bound).astype(held_as)


def setup_inputs(seed: int = 0) -> dict:
    keys = jax.random.split(jax.random.key(seed), 12)
    emb_table = centred(keys[0], (VOCAB, E), 0.5, 3.0, ((0, 16),), jnp.float32)
    row_accum = jnp.clip(jnp.exp(math.log(1.0) - 6.9077552 * jax.random.uniform(keys[1], (VOCAB,), jnp.float32) ** shard_levels(keys[1], (VOCAB,), ((0, 16),), -0.2, 0.2)), 0.001, 1.0)
    look_rows = touch_ends(ranked(keys[2], (N_REPLICA, N_TABLE, N_TABLE, HOT, CAP), ROWS_DEV, 2), jax.random.fold_in(keys[2], 3), 0, ROWS_DEV - 1).astype(jnp.int32)
    live_counts = jax.vmap(lambda own: ragged(own, N_TABLE, K, CAP, 2))(jax.random.split(keys[3], N_REPLICA * N_TABLE)).reshape((N_REPLICA, N_TABLE, N_TABLE)).astype(jnp.int32)
    bag_order = jax.vmap(lambda own: jax.random.permutation(own, K))(jax.random.split(keys[4], N_REPLICA * N_TABLE)).reshape((N_REPLICA, N_TABLE, K)).astype(jnp.int32)
    dense_emb = centred(keys[5], (SAMPLES, E), 1.0, 6.0, ((0, 512),))
    labels = touch_ends((jax.random.randint(keys[6], (SAMPLES,), 0, 4) < 1).astype(jnp.int32), jax.random.fold_in(keys[6], 1), 0, 1)
    cross_in = centred(keys[7], (D, RANK), D ** -0.5, 0.109375, ((0, 16),))
    cross_out = centred(keys[8], (D, RANK), RANK ** -0.5, 0.25, ((0, 16),))
    cross_bias = centred(keys[9], (D,), 0.5, 3.0, (), jnp.float32)
    head_weight = centred(keys[10], (D,), D ** -0.5, 0.109375, (), jnp.float32)
    return {"emb_table": emb_table, "row_accum": row_accum, "look_rows": look_rows, "live_counts": live_counts, "bag_order": bag_order, "dense_emb": dense_emb, "labels": labels, "cross_in": cross_in, "cross_out": cross_out, "cross_bias": cross_bias, "head_weight": head_weight}


EPSILON = 1e-08

def bag_sources(live_row, permute, capacity):
    bag_count = permute.shape[0]
    slot_ends = jnp.cumsum(live_row).astype(jnp.int32)
    counter = jnp.arange(bag_count, dtype=jnp.int32)
    passed = (counter[:, None] >= slot_ends[None, :]).astype(jnp.int32)
    source = lax.optimization_barrier(jnp.sum(passed, axis=1)).astype(jnp.int32)
    before = lax.optimization_barrier(jnp.sum(passed * live_row[None, :], axis=1)).astype(jnp.int32)
    flat_slot = source * capacity + (counter - before)
    inverse = jnp.zeros((bag_count,), jnp.int32).at[permute].set(counter)
    return flat_slot[inverse].astype(jnp.int32)

def slot_bags(live_row, permute, capacity):
    bag_count = permute.shape[0]
    starts = (jnp.cumsum(live_row) - live_row).astype(jnp.int32)
    column = jnp.arange(capacity, dtype=jnp.int32)
    position = jnp.minimum(starts[:, None] + column[None, :], bag_count - 1).astype(jnp.int32)
    is_live = column[None, :] < live_row[:, None]
    return (permute[position], is_live)

def reference(emb_table, row_accum, look_rows, live_counts, bag_order, dense_emb, labels, cross_in, cross_out, cross_bias, head_weight):
    replicas = look_rows.shape[0]
    shards = look_rows.shape[1]
    capacity = look_rows.shape[4]
    feature_width = emb_table.shape[1]
    rows_dev = emb_table.shape[0] // shards
    batch_size = dense_emb.shape[0] // (replicas * shards)
    shard_tables = emb_table.reshape(shards, rows_dev, feature_width)
    dense_all = dense_emb.reshape(replicas, shards * batch_size, feature_width)
    label_all = labels.reshape(replicas, shards * batch_size).astype(jnp.float32)
    contract = (((1,), (1,)), ((), ()))

    def one_replica(grad_sum, inputs):
        row_ids, live_rep, order_rep, dense_rep, label_rep = inputs

        def pool_source(shard_rows, source_ids):
            picked = jnp.take(shard_rows, source_ids, axis=0)
            return lax.optimization_barrier(jnp.sum(picked, axis=1)).astype(jnp.bfloat16)
        slot_pool = jax.vmap(pool_source)(shard_tables, row_ids)

        def gather_dest(dest_slots, live_row, permute):
            bag_slot = bag_sources(live_row, permute, capacity)
            return jnp.take(dest_slots.reshape(-1, feature_width), bag_slot, axis=0)
        pooled = jax.vmap(gather_dest, in_axes=(1, 0, 0))(slot_pool, live_rep, order_rep)
        pooled = pooled.reshape(shards * batch_size, -1)
        cross_input = jnp.concatenate([dense_rep, pooled], axis=1)
        hidden = jnp.dot(cross_input, cross_in, preferred_element_type=jnp.float32).astype(jnp.bfloat16)
        mixed_rows = lax.dot_general(hidden, cross_out, contract, preferred_element_type=jnp.float32) + cross_bias
        crossed = cross_input * mixed_rows + cross_input
        logits = jnp.dot(crossed, head_weight, precision=lax.Precision.HIGHEST)
        logit_grad = jax.nn.sigmoid(logits) - label_rep
        cross_grad = logit_grad[:, None] * head_weight[None, :]
        mixed_grad = (cross_grad * cross_input).astype(jnp.bfloat16)
        hidden_grad = jnp.dot(mixed_grad, cross_out, preferred_element_type=jnp.float32).astype(jnp.bfloat16)
        input_grad = cross_grad * (mixed_rows + 1.0) + lax.dot_general(hidden_grad, cross_in, contract, preferred_element_type=jnp.float32)
        pooled_grad = input_grad[:, feature_width:].astype(jnp.bfloat16).reshape(shards, -1, feature_width)

        def back_dest(bag_grads, live_row, permute):
            bag_ids, is_live = slot_bags(live_row, permute, capacity)
            picked = jnp.take(bag_grads, bag_ids.reshape(-1), axis=0).reshape(shards, capacity, feature_width)
            return jnp.where(is_live[:, :, None], picked, jnp.zeros_like(picked))
        slot_grads = jax.vmap(back_dest)(pooled_grad, live_rep, order_rep)
        global_ids = row_ids + (jnp.arange(shards, dtype=jnp.int32) * rows_dev)[:, None, None, None]
        values = jnp.transpose(slot_grads, (1, 0, 2, 3))[:, :, None, :, :].astype(jnp.float32)
        values = jnp.broadcast_to(values, global_ids.shape + (feature_width,))
        grad_sum = grad_sum.at[global_ids.reshape(-1)].add(values.reshape(-1, feature_width))
        return (grad_sum, logits)
    start_grads = jnp.zeros(emb_table.shape, jnp.float32)
    row_grad, logits = lax.scan(one_replica, start_grads, (look_rows, live_counts, bag_order, dense_all, label_all))
    new_accum = row_accum + lax.optimization_barrier(jnp.mean(row_grad * row_grad, axis=1))
    row_update = -row_grad / (jnp.sqrt(new_accum)[:, None] + EPSILON)
    return (logits.reshape(-1), row_update, new_accum)
```

```python
import jax
import jax.numpy as jnp
from jax import lax
from jax.experimental import pallas as pl
from jax.experimental.pallas import tpu as pltpu
from jax.sharding import PartitionSpec as P

EPSILON = 1e-08
MESH = pl.DeviceIdType.MESH
CHUNK = 384
BLOCK = 256


def multi_hot(ids, rows, store):
    hot, n = ids.shape
    row = lax.broadcasted_iota(jnp.int32, (BLOCK, n), 0).astype(jnp.float32).astype(jnp.bfloat16)
    one = jnp.ones((BLOCK, n), jnp.bfloat16)
    zero = jnp.zeros((BLOCK, n), jnp.bfloat16)
    for first in range(0, rows, BLOCK):
        near = jnp.clip(ids - first, -1, BLOCK).astype(jnp.float32).astype(jnp.bfloat16)
        total = None
        for member in range(hot):
            hit = jnp.where(row == near[member : member + 1, :], one, zero)
            total = hit if total is None else total + hit
        store(first, total)


def pool_kernel(ids_ref, table_ref, out_ref, table_t, hits):
    rows = table_ref.shape[0]
    width = table_ref.shape[1]

    @pl.when(pl.program_id(0) == 0)
    def _():
        turned = table_ref[...].T
        high = turned.astype(jnp.bfloat16)
        table_t[:width, :] = high
        table_t[width:, :] = (turned - high.astype(jnp.float32)).astype(jnp.bfloat16)

    def store(first, block):
        hits[first : first + BLOCK, :] = block

    multi_hot(ids_ref[...], rows, store)
    both = jnp.dot(table_t[...], hits[...], preferred_element_type=jnp.float32)
    out_ref[...] = (both[:width, :] + both[width:, :]).T.astype(jnp.bfloat16)


def pool(ids, table):
    hot, slots = ids.shape
    rows, width = table.shape
    return pl.pallas_call(
        pool_kernel,
        grid=(slots // CHUNK,),
        in_specs=[
            pl.BlockSpec((hot, CHUNK), lambda i: (0, i)),
            pl.BlockSpec((rows, width), lambda i: (0, 0)),
        ],
        out_specs=pl.BlockSpec((CHUNK, width), lambda i: (i, 0)),
        out_shape=jax.ShapeDtypeStruct((slots, width), jnp.bfloat16),
        scratch_shapes=[
            pltpu.VMEM((2 * width, rows), jnp.bfloat16),
            pltpu.VMEM((rows, CHUNK), jnp.bfloat16),
        ],
        name="pool",
    )(ids, table)


def finish_kernel(
    ids_ref, outgoing_ref, accum_ref, update_ref, squares_ref,
    arrived, hits, grads, parts, result,
    back_send, back_recv, part_send, part_recv, result_send, result_recv, own_sem,
):
    shards, capacity, width = outgoing_ref.shape
    padded = arrived.shape[1]
    copies, share, _ = grads.shape
    rows = copies * share
    own_table = lax.axis_index("table")
    own_copy = lax.axis_index("replica")

    barrier = pltpu.get_barrier_semaphore()

    def greet_table(d, carry):
        pl.semaphore_signal(barrier, inc=1, device_id=(own_copy, lax.rem(own_table + d, shards)), device_id_type=MESH)
        return carry

    def greet_copy(d, carry):
        pl.semaphore_signal(barrier, inc=1, device_id=(lax.rem(own_copy + d, copies), own_table), device_id_type=MESH)
        return carry

    lax.fori_loop(1, shards, greet_table, 0)
    lax.fori_loop(1, copies, greet_copy, 0)
    pl.semaphore_wait(barrier, shards + copies - 2)

    def back(d):
        peer = lax.rem(own_table + d, shards)
        return pltpu.make_async_remote_copy(
            src_ref=outgoing_ref.at[peer],
            dst_ref=arrived.at[own_table, pl.ds(0, capacity)],
            send_sem=back_send.at[d],
            recv_sem=back_recv.at[d],
            device_id=(own_copy, peer),
            device_id_type=MESH,
        )

    def start_back(d, carry):
        back(d).start()
        return carry

    lax.fori_loop(1, shards, start_back, 0)
    own = pltpu.make_async_copy(outgoing_ref.at[own_table], arrived.at[own_table, pl.ds(0, capacity)], own_sem)
    own.start()

    def prepare(s, carry):
        arrived[s, pl.ds(capacity, padded - capacity), :] = jnp.zeros((padded - capacity, width), jnp.bfloat16)

        def store(first, block):
            hits[s, first : first + BLOCK, :] = block

        multi_hot(ids_ref[s], rows, store)
        return carry

    lax.fori_loop(0, shards, prepare, 0)
    own.wait()
    grads[...] = jnp.dot(hits[own_table], arrived[own_table], preferred_element_type=jnp.float32).reshape(grads.shape)

    def add(d, carry):
        source = lax.rem(own_table + shards - d, shards)
        back(d).wait_recv()
        term = jnp.dot(hits[source], arrived[source], preferred_element_type=jnp.float32)
        grads[...] += term.reshape(grads.shape)
        return carry

    lax.fori_loop(1, shards, add, 0)

    def part(d):
        peer = lax.rem(own_copy + d, copies)
        return pltpu.make_async_remote_copy(
            src_ref=grads.at[peer],
            dst_ref=parts.at[d],
            send_sem=part_send.at[d],
            recv_sem=part_recv.at[d],
            device_id=(peer, own_table),
            device_id_type=MESH,
        )

    def start_part(d, carry):
        part(d).start()
        return carry

    lax.fori_loop(1, copies, start_part, 0)

    def add_part(d, total):
        part(d).wait_recv()
        return total + parts[d]

    total = lax.fori_loop(1, copies, add_part, grads[own_copy])
    diagonal = lax.broadcasted_iota(jnp.int32, (share, width), 0) == lax.broadcasted_iota(jnp.int32, (share, width), 1)
    before = jnp.sum(jnp.where(diagonal, accum_ref[pl.ds(own_copy, 1), :], 0.0), axis=1, keepdims=True)
    accum = before + jnp.sum(total * total, axis=1, keepdims=True) * (1.0 / width)
    result[own_copy, :share, :] = -total / (jnp.sqrt(accum) + EPSILON)
    squares = jnp.sum(jnp.where(diagonal, accum, 0.0), axis=0, keepdims=True)
    result[own_copy, pl.ds(share, 8), :] = jnp.broadcast_to(squares, (8, width))

    def share_out(d):
        peer = lax.rem(own_copy + d, copies)
        return pltpu.make_async_remote_copy(
            src_ref=result.at[own_copy],
            dst_ref=result.at[own_copy],
            send_sem=result_send.at[d],
            recv_sem=result_recv.at[d],
            device_id=(peer, own_table),
            device_id_type=MESH,
        )

    def start_share(d, carry):
        share_out(d).start()
        return carry

    lax.fori_loop(1, copies, start_share, 0)

    def write(source):
        update_ref[source] = result[source, :share, :]
        squares_ref[pl.ds(source, 1), :] = result[source, pl.ds(share, 1), :]

    write(own_copy)

    def take(d, carry):
        share_out(d).wait_recv()
        write(lax.rem(own_copy + copies - d, copies))
        return carry

    lax.fori_loop(1, copies, take, 0)

    def sent_back(d, carry):
        back(d).wait_send()
        return carry

    def sent_copy(d, carry):
        part(d).wait_send()
        share_out(d).wait_send()
        return carry

    lax.fori_loop(1, shards, sent_back, 0)
    lax.fori_loop(1, copies, sent_copy, 0)


def finish(ids, outgoing, accum, rows, copies):
    shards, hot, padded = ids.shape
    width = outgoing.shape[2]
    capacity = outgoing.shape[1]
    share = rows // copies
    vmem = pl.BlockSpec(memory_space=pltpu.VMEM)
    return pl.pallas_call(
        finish_kernel,
        in_specs=[vmem] * 3,
        out_specs=[vmem] * 2,
        out_shape=[
            jax.ShapeDtypeStruct((copies, share, width), jnp.float32),
            jax.ShapeDtypeStruct((copies, width), jnp.float32),
        ],
        scratch_shapes=[
            pltpu.VMEM((shards, padded, width), jnp.bfloat16),
            pltpu.VMEM((shards, rows, padded), jnp.bfloat16),
            pltpu.VMEM((copies, share, width), jnp.float32),
            pltpu.VMEM((copies, share, width), jnp.float32),
            pltpu.VMEM((copies, share + 8, width), jnp.float32),
            pltpu.SemaphoreType.DMA((shards,)),
            pltpu.SemaphoreType.DMA((shards,)),
            pltpu.SemaphoreType.DMA((copies,)),
            pltpu.SemaphoreType.DMA((copies,)),
            pltpu.SemaphoreType.DMA((copies,)),
            pltpu.SemaphoreType.DMA((copies,)),
            pltpu.SemaphoreType.DMA,
        ],
        compiler_params=pltpu.CompilerParams(collective_id=1, has_side_effects=True),
        name="finish",
    )(ids, outgoing, accum)


def cross_kernel(
    place_ref, live_ref, start_ref, arrived_ref, dense_ref, labels_ref, in_hbm, out_hbm, bias_ref, head_ref,
    logits_ref, outgoing_ref,
    slots, bags, inputs, mixed, scaled, w_in, w_out, sems,
):
    shards, capacity, width = arrived_ref.shape
    batch = dense_ref.shape[0]
    features = inputs.shape[1] // width - 1
    load_in = pltpu.make_async_copy(in_hbm, w_in, sems.at[0])
    load_out = pltpu.make_async_copy(out_hbm, w_out, sems.at[1])
    load_in.start()
    load_out.start()

    def widen(s, carry):
        first = pl.multiple_of(s * capacity, 8)
        slots[pl.ds(first, capacity), :] = arrived_ref[s].astype(jnp.float32)
        return carry

    lax.fori_loop(0, shards, widen, 0)

    def arrange(s, carry):
        base = start_ref[s]

        def eight(i, inner):
            row = pl.multiple_of(s * capacity + i * 8, 8)
            for j in range(8):
                bags[pl.ds(place_ref[base + i * 8 + j], 1), :] = slots[pl.ds(row + j, 1), :]
            return inner

        lax.fori_loop(0, (live_ref[s] + 7) // 8, eight, 0)
        return carry

    lax.fori_loop(0, shards, arrange, 0)

    inputs[:, :width] = dense_ref[...]
    for f in range(features):
        inputs[:, (f + 1) * width : (f + 2) * width] = bags[f * batch : (f + 1) * batch, :].astype(jnp.bfloat16)

    rank = w_in.shape[1]
    columns = inputs.shape[1]
    step = 3 * width
    contract = (((1,), (1,)), ((), ()))
    load_in.wait()
    hidden = jnp.dot(inputs[...], w_in[...], preferred_element_type=jnp.float32).astype(jnp.bfloat16)
    load_out.wait()
    total = jnp.zeros((batch, 1), jnp.float32)
    for first in range(0, columns, step):
        part = slice(first, first + step)
        x = inputs[:, part].astype(jnp.float32)
        m = lax.dot_general(hidden, w_out[part, :], contract, preferred_element_type=jnp.float32) + bias_ref[:, part]
        mixed[:, part] = m
        total = total + jnp.sum((x * m + x) * head_ref[:, part], axis=1, keepdims=True)
    diagonal = lax.broadcasted_iota(jnp.int32, (batch, batch), 0) == lax.broadcasted_iota(jnp.int32, (batch, batch), 1)
    logits_ref[...] = jnp.sum(jnp.where(diagonal, total, 0.0), axis=0, keepdims=True)
    marks = jnp.sum(jnp.where(diagonal, labels_ref[...].astype(jnp.float32), 0.0), axis=1, keepdims=True)
    slope = 1.0 / (1.0 + jnp.exp(-total)) - marks
    for first in range(0, columns, step):
        part = slice(first, first + step)
        x = inputs[:, part].astype(jnp.float32)
        scaled[:, part] = (slope * head_ref[:, part] * x).astype(jnp.bfloat16)
    hidden_grad = jnp.dot(scaled[...], w_out[...], preferred_element_type=jnp.float32).astype(jnp.bfloat16)
    for first in range(width, columns, 2 * width):
        part = slice(first, first + 2 * width)
        back = lax.dot_general(hidden_grad, w_in[part, :], contract, preferred_element_type=jnp.float32)
        grad = slope * head_ref[:, part] * (mixed[:, part] + 1.0) + back
        row = (first // width - 1) * batch
        bags[row : row + batch, :] = grad[:, :width]
        bags[row + batch : row + 2 * batch, :] = grad[:, width:]

    def collect(s, carry):
        base = start_ref[s]

        def eight(i, inner):
            row = pl.multiple_of(s * capacity + i * 8, 8)
            for j in range(8):
                slots[pl.ds(row + j, 1), :] = bags[pl.ds(place_ref[base + i * 8 + j], 1), :]
            return inner

        lax.fori_loop(0, (live_ref[s] + 7) // 8, eight, 0)
        return carry

    lax.fori_loop(0, shards, collect, 0)
    which = lax.broadcasted_iota(jnp.int32, (capacity, width), 0)

    def narrow(s, carry):
        first = pl.multiple_of(s * capacity, 8)
        value = slots[pl.ds(first, capacity), :]
        outgoing_ref[s] = jnp.where(which < live_ref[s], value, 0.0).astype(jnp.bfloat16)
        return carry

    lax.fori_loop(0, shards, narrow, 0)


def cross(place, live, start, arrived, dense, labels, full_in, full_out, bias, head):
    shards, capacity, width = arrived.shape
    batch = dense.shape[0]
    columns, rank = full_in.shape
    features = columns // width - 1
    vmem = pl.BlockSpec(memory_space=pltpu.VMEM)
    smem = pl.BlockSpec(memory_space=pltpu.SMEM)
    hbm = pl.BlockSpec(memory_space=pl.ANY)
    return pl.pallas_call(
        cross_kernel,
        in_specs=[smem, smem, smem, vmem, vmem, vmem, hbm, hbm, vmem, vmem],
        out_specs=[vmem, vmem],
        out_shape=[
            jax.ShapeDtypeStruct((1, batch), jnp.float32),
            jax.ShapeDtypeStruct((shards, capacity, width), jnp.bfloat16),
        ],
        scratch_shapes=[
            pltpu.VMEM((shards * capacity, width), jnp.float32),
            pltpu.VMEM((features * batch + 8, width), jnp.float32),
            pltpu.VMEM((batch, columns), jnp.bfloat16),
            pltpu.VMEM((batch, columns), jnp.float32),
            pltpu.VMEM((batch, columns), jnp.bfloat16),
            pltpu.VMEM((columns, rank), jnp.bfloat16),
            pltpu.VMEM((columns, rank), jnp.bfloat16),
            pltpu.SemaphoreType.DMA((2,)),
        ],
        name="cross",
    )(place, live, start, arrived, dense, labels, full_in, full_out, bias, head)


def local(
    emb_table,
    row_accum,
    look_rows,
    live_counts,
    bag_order,
    dense_emb,
    labels,
    cross_in,
    cross_out,
    cross_bias,
    head_weight,
):
    shards = lax.axis_size("table")
    copies = lax.axis_size("replica")
    own_index = lax.axis_index("table")
    rows, width = emb_table.shape
    hot, capacity = look_rows.shape[3:]
    batch = dense_emb.shape[0]
    features = cross_in.shape[0] * shards // width - 1
    ids = look_rows[0, 0].transpose(1, 0, 2).reshape(hot, shards * capacity)
    pooled = pool(ids, emb_table).reshape(shards, capacity, width)
    arrived = lax.all_to_all(pooled, "table", split_axis=0, concat_axis=0, tiled=True)
    live = lax.dynamic_index_in_dim(live_counts[0], own_index, 0, keepdims=False)
    start = jnp.cumsum(live) - live
    order = bag_order[0, 0]
    place = order % features * batch + order // features
    place = jnp.pad(place, (0, 8), constant_values=features * batch)
    full_in = lax.all_gather(cross_in, "table", axis=0, tiled=True)
    full_out = lax.all_gather(cross_out, "table", axis=0, tiled=True)
    logits, outgoing = cross(
        place, live, start, arrived, dense_emb, labels.reshape(1, -1), full_in, full_out,
        cross_bias.reshape(1, -1), head_weight.reshape(1, -1),
    )
    padded = -(-capacity // 128) * 128
    lanes = jnp.pad(look_rows[0, 0], ((0, 0), (0, 0), (0, padded - capacity)), constant_values=-1)
    accum = jnp.pad(row_accum.reshape(copies, rows // copies), ((0, 0), (0, width - rows // copies)))
    update, squares = finish(lanes, outgoing, accum, rows, copies)
    row_update = update.reshape(rows, width)
    new_accum = squares[:, : rows // copies].reshape(rows)
    return (logits.reshape(-1), row_update, new_accum)


def solution(mesh):
    placed = (
        P("table", None),
        P("table"),
        P("replica", "table", None, None, None),
        P("replica", None, None),
        P("replica", "table", None),
        P(("replica", "table"), None),
        P(("replica", "table")),
        P("table", None),
        P("table", None),
        P(),
        P(),
    )
    return jax.shard_map(
        local,
        mesh=mesh,
        in_specs=placed,
        out_specs=(P(("replica", "table")), P("table", None), P("table")),
        check_vma=False,
    )
```
